32 devices in a mesh: energy: 4 (over z), rows: 8 (over y, x, core).
Axes of the slice: x: 2, y: 2, z: 4, core: 2. Of those that a mesh axis runs over, the one named last changes fastest.
Arguments:
- coupling: bfloat16 [2, 512, 512], replicated, may hold values from -4.1875 to 4.1875
- inverses: bfloat16 [32, 4, 2, 256, 256], P(('energy', 'rows')), may hold values from -0.0078125 to 0.0078125
- contact_row: int32 [12], replicated, may hold values from 0 to 7, as said below
- assignment: int32 [8], P('energy'), may hold values from 0 to 7, as said below
- states: bfloat16 [12, 2, 16, 512], replicated, may hold values from -0.119628906 to 0.119628906
- weights: float32 [8], P('energy'), may hold values from 0.03 to 0.3
Outputs:
- injection: float32 [8, 8, 2, 16, 512], P('energy', 'rows')
- integrated: float32 [8, 2, 16, 512], P('rows')
- far_forward: bfloat16 [32, 2, 256, 256], P(('energy', 'rows'))
- far_backward: bfloat16 [32, 2, 256, 256], P(('energy', 'rows'))
The draws below stay inside these ranges and needn't reach their ends.
Inputs may be any that keep to these rules, and one draw needn't show every extreme that they name: `contact_row`: every device block row has one contact or more. `assignment`: each aligned block of 2 entries, b * 2 to b * 2 + 1, holds each of those same numbers once.
All inputs are finite; a program needn't handle non-finite values.
Results may differ from the reference program's by a relative error of at most 0.024.
Values may be sent and summed in bfloat16 or wider, within the bound.
A program may use at most 64 MiB of HBM per device.

```python
import math
import jax
import jax.numpy as jnp
from jax import lax

ORBITALS = 512
ITERS = 4
STATES = 16
HALF = 256
GROUPS = 2
ENERGIES = 8
QUARTERS = 32
BLOCK_ROWS = 8
CONTACTS = 12


def draw_contact_row(key, part):
    first_key, second_key, third_key = jax.random.split(jax.random.fold_in(key, 11), 3)
    covering = jax.random.permutation(first_key, BLOCK_ROWS).astype(jnp.int32)
    extra_rows = jax.random.randint(second_key, (CONTACTS - BLOCK_ROWS,), 0, BLOCK_ROWS).astype(jnp.int32)
    joined = jnp.concatenate([covering, extra_rows])
    shuffle = jax.random.permutation(third_key, CONTACTS)
    return jnp.take(joined, shuffle).astype(jnp.int32)


def block_permutation(block_key):
    return jax.random.permutation(block_key, GROUPS).astype(jnp.int32)


def draw_assignment(key, part):
    block_keys = jax.random.split(jax.random.fold_in(key, 23), ENERGIES // GROUPS)
    blocks = jax.vmap(block_permutation)(block_keys)
    offsets = (jnp.arange(ENERGIES // GROUPS, dtype=jnp.int32) * GROUPS)[:, None]
    return (blocks + offsets).reshape(ENERGIES).astype(jnp.int32)


def block_scale(stream_key, shape, shards, low, top_value):
    level, own = 1.0, jax.random.fold_in(stream_key, 6)
    for dim, parts in shards:
        draws = jnp.exp(jax.random.uniform(jax.random.fold_in(own, dim), (parts,), jnp.float32, low / len(shards), top_value / len(shards)))
        level = level * jnp.repeat(draws, shape[dim] // parts).reshape([-1 if axis == dim else 1 for axis in range(len(shape))])
    return level


def normal_values(stream_key, shape, width, most, shards=(), kind=jnp.bfloat16):
    array = jax.random.normal(stream_key, shape, jnp.float32) * width
    if len(shards) > 0:
        array = block_scale(stream_key, shape, shards, -0.22, 0.18) * array
    return jnp.clip(array, min=-most, max=most).astype(kind)


def setup_inputs(seed: int = 0) -> dict:
    key_list = jax.random.split(jax.random.key(seed), 7)
    coupling = normal_values(key_list[0], (2, ORBITALS, ORBITALS), 0.7, 4.1875)
    inverses = normal_values(key_list[1], (QUARTERS, ITERS, 2, HALF, HALF), (2 * ORBITALS * ORBITALS) ** -0.5, 0.0078125, ((0, 32),))
    contact_row = draw_contact_row(jax.random.fold_in(key_list[6], 71), 0)
    assignment = draw_assignment(jax.random.fold_in(key_list[6], 71), 0)
    states = normal_values(key_list[4], (CONTACTS, 2, STATES, ORBITALS), 0.02, 0.119628906)
    weights = jnp.clip(jnp.exp(math.log(0.3) - 2.3025852 * jax.random.uniform(key_list[5], (ENERGIES,), jnp.float32) ** block_scale(key_list[5], (ENERGIES,), ((0, 4),), -0.2, 0.2)), 0.03, 0.3)
    return {"coupling": coupling, "inverses": inverses, "contact_row": contact_row, "assignment": assignment, "states": states, "weights": weights}


def complex_dot(left_matrix, right_matrix):
    def single(leading, trailing):
        return jnp.dot(leading.astype(jnp.float32), trailing.astype(jnp.float32), preferred_element_type=jnp.float32)
    real_part = single(left_matrix[0], right_matrix[0]) - single(left_matrix[1], right_matrix[1])
    imag_part = single(left_matrix[0], right_matrix[1]) + single(left_matrix[1], right_matrix[0])
    return jnp.stack([real_part, imag_part])


def reference(coupling, inverses, contact_row, assignment, states, weights):
    half_order = ORBITALS // 2

    def assemble(blocks):
        shaped = blocks.reshape(2, 2, ITERS, 2, half_order, half_order)
        return shaped.transpose(2, 3, 0, 4, 1, 5).reshape(ITERS, 2, ORBITALS, ORBITALS)

    def split_blocks(matrix):
        shaped = matrix.reshape(2, 2, half_order, 2, half_order)
        return shaped.transpose(1, 3, 0, 2, 4).reshape(4, 2, half_order, half_order)

    forward_start = coupling
    backward_start = jnp.stack([coupling[0].T, -coupling[1].T])
    row_ids = jnp.arange(BLOCK_ROWS, dtype=jnp.int32)
    selector = (contact_row[None, :] == row_ids[:, None]).astype(jnp.float32)
    drive = jnp.dot(selector, states.reshape(CONTACTS, -1).astype(jnp.float32), preferred_element_type=jnp.float32)
    drive = drive.astype(jnp.bfloat16).reshape(BLOCK_ROWS, 2, STATES, ORBITALS)
    drive_real = drive[:, 0].reshape(BLOCK_ROWS * STATES, ORBITALS).astype(jnp.float32)
    drive_imag = drive[:, 1].reshape(BLOCK_ROWS * STATES, ORBITALS).astype(jnp.float32)

    def per_slot(blocks):
        inverse_all = assemble(blocks)
        forward = forward_start
        backward = backward_start
        surface_sum = jnp.zeros((2, ORBITALS, ORBITALS), jnp.float32)
        for iteration in range(ITERS):
            forward_green = complex_dot(forward, inverse_all[iteration]).astype(jnp.bfloat16)
            backward_green = complex_dot(backward, inverse_all[iteration]).astype(jnp.bfloat16)
            surface_sum = surface_sum + complex_dot(forward_green, backward)
            forward_next = complex_dot(forward_green, forward).astype(jnp.bfloat16)
            backward = complex_dot(backward_green, backward).astype(jnp.bfloat16)
            forward = forward_next
        self_energy = surface_sum.astype(jnp.bfloat16).astype(jnp.float32)
        energy_real = self_energy[0].T
        energy_imag = self_energy[1].T
        real_part = jnp.dot(drive_real, energy_real, preferred_element_type=jnp.float32) - jnp.dot(drive_imag, energy_imag, preferred_element_type=jnp.float32)
        imag_part = jnp.dot(drive_imag, energy_real, preferred_element_type=jnp.float32) + jnp.dot(drive_real, energy_imag, preferred_element_type=jnp.float32)
        injected = jnp.stack([real_part.reshape(BLOCK_ROWS, STATES, ORBITALS), imag_part.reshape(BLOCK_ROWS, STATES, ORBITALS)], axis=1)
        return injected, split_blocks(forward), split_blocks(backward)

    slot_blocks = inverses.reshape(ENERGIES, 4, ITERS, 2, half_order, half_order)
    slot_injection, far_fwd, far_bwd = lax.map(per_slot, slot_blocks)
    injection = jnp.zeros_like(slot_injection).at[assignment].set(slot_injection)
    integrated = jnp.tensordot(weights, injection, axes=1, precision=lax.Precision.HIGHEST)
    far_forward = far_fwd.reshape(QUARTERS, 2, half_order, half_order)
    far_backward = far_bwd.reshape(QUARTERS, 2, half_order, half_order)
    return injection, integrated, far_forward, far_backward
```

```python
import functools

import jax
import jax.numpy as jnp
from jax import lax
from jax.experimental import pallas as pl
from jax.experimental.pallas import tpu as pltpu
from jax.sharding import PartitionSpec as P

MESH = pl.DeviceIdType.MESH
BF16 = jnp.bfloat16
F32 = jnp.float32


def remote(src, dst, send_sem, recv_sem, axis, target):
    return pltpu.make_async_remote_copy(
        src_ref=src,
        dst_ref=dst,
        send_sem=send_sem,
        recv_sem=recv_sem,
        device_id={axis: target},
        device_id_type=MESH,
    )


def mul(left, right):
    return jnp.dot(left, right, preferred_element_type=F32)


def kernel(
    rows_size,
    energy_size,
    coupling_ref,
    inverses_ref,
    contact_ref,
    assignment_ref,
    states_ref,
    weights_ref,
    injection_ref,
    integrated_ref,
    far_forward_ref,
    far_backward_ref,
    held,
    blocks,
    chain,
    product,
    right_chain,
    right_green,
    arrived,
    surface,
    drive,
    pieces,
    gathered,
    weighted,
    over_energy,
    stage,
    local_sems,
    cross_sems,
    core_sems,
    relay_sems,
    product_sems,
    far_sems,
    piece_send,
    piece_recv,
    energy_send,
    energy_recv,
):
    energy = lax.axis_index("energy")
    position = lax.axis_index("rows")
    iters = inverses_ref.shape[1]
    half = inverses_ref.shape[-1]
    whole = 2 * half
    groups = assignment_ref.shape[0]
    contacts, _, states_count, _ = states_ref.shape
    slot = position // 4
    row_bit = position // 2 % 2
    column_bit = position % 2
    across = slot * 4 + 2 * (1 - row_bit) + column_bit
    beside = slot * 4 + 2 * row_bit + 1 - column_bit
    own_block = 2 * row_bit + column_bit
    cross_block = 2 * (1 - row_bit) + column_bit

    load_coupling = pltpu.make_async_copy(coupling_ref, held, local_sems.at[0])
    load_coupling.start()
    load_inverse = pltpu.make_async_copy(
        inverses_ref.at[0], blocks.at[own_block], local_sems.at[1]
    )
    load_inverse.start()

    barrier = pltpu.get_barrier_semaphore()
    for step in range(1, rows_size):
        pl.semaphore_signal(
            barrier,
            inc=1,
            device_id={"rows": lax.rem(position + step, rows_size)},
            device_id_type=MESH,
        )
    for step in range(1, energy_size):
        pl.semaphore_signal(
            barrier,
            inc=1,
            device_id={"energy": lax.rem(energy + step, energy_size)},
            device_id_type=MESH,
        )
    pl.semaphore_wait(barrier, rows_size + energy_size - 2)

    cross = [
        remote(
            inverses_ref.at[0, k],
            blocks.at[own_block, k],
            cross_sems.at[0, k],
            cross_sems.at[1, k],
            "rows",
            across,
        )
        for k in range(iters)
    ]
    core = [
        remote(
            inverses_ref.at[0, k],
            blocks.at[own_block, k],
            core_sems.at[0, k],
            core_sems.at[1, k],
            "rows",
            beside,
        )
        for k in range(iters)
    ]
    relay = [
        remote(
            blocks.at[cross_block, k],
            blocks.at[cross_block, k],
            relay_sems.at[0, k],
            relay_sems.at[1, k],
            "rows",
            beside,
        )
        for k in range(iters)
    ]
    strip = pl.ds(pl.multiple_of(row_bit * half, half), half)
    share = [
        remote(
            product.at[k, strip],
            arrived.at[k],
            product_sems.at[0, k],
            product_sems.at[1, k],
            "rows",
            beside,
        )
        for k in range(iters)
    ]
    for k in range(iters):
        cross[k].start()
    for k in range(min(2, iters)):
        core[k].start()

    load_coupling.wait()

    def spread(part, index):
        for block in range(2):
            chain[:, pl.ds(block * whole + index * half, half)] = part[
                :, block * half : (block + 1) * half
            ]

    @pl.when(column_bit == 0)
    def _():
        spread(held[0], 0)
        spread(held[1], 1)

    @pl.when(column_bit == 1)
    def _():
        spread(held[0].T, 0)
        spread(-(held[1].T), 1)

    def build_chain(k):
        for block in range(2):
            for line in range(2):
                lines = slice(line * half, (line + 1) * half)
                real = chain[lines, block * whole : block * whole + half]
                imag = chain[lines, block * whole + half : (block + 1) * whole]
                top = line * whole
                right_chain[k, block, top : top + half, :half] = real
                right_chain[k, block, top : top + half, half:] = imag
                right_chain[k, block, top + half : top + whole, :half] = -imag
                right_chain[k, block, top + half : top + whole, half:] = real

    def build_green(k, block):
        for line in range(2):
            real = blocks[2 * line + block, k, 0]
            imag = blocks[2 * line + block, k, 1]
            top = line * whole
            right_green[top : top + half, :half] = real
            right_green[top : top + half, half:] = imag
            right_green[top + half : top + whole, :half] = -imag
            right_green[top + half : top + whole, half:] = real

    build_chain(0)

    per_row = 2 * states_count
    shift = per_row.bit_length() - 1
    shape = (rows_size * per_row, contacts * per_row)
    line_ids = lax.broadcasted_iota(jnp.int32, shape, 0)
    lane_ids = lax.broadcasted_iota(jnp.int32, shape, 1)
    lane_contact = lane_ids >> shift
    lane_row = jnp.zeros(shape, jnp.int32)
    for contact in range(contacts):
        lane_row = jnp.where(lane_contact == contact, contact_ref[contact], lane_row)
    chosen = lane_row == (line_ids >> shift)
    line_item = line_ids & (per_row - 1)
    lane_item = lane_ids & (per_row - 1)
    flat_states = states_ref[...].reshape(contacts * per_row, whole)
    straight = jnp.where(chosen & (line_item == lane_item), 1.0, 0.0).astype(BF16)
    turned_item = (line_item + states_count) & (per_row - 1)
    sign = jnp.where(line_item < states_count, -1.0, 1.0)
    turned = jnp.where(chosen & (turned_item == lane_item), sign, 0.0).astype(BF16)
    drive_straight = mul(straight, flat_states).astype(BF16)
    drive_turned = mul(turned, flat_states).astype(BF16)
    for block in range(2):
        lanes = slice(block * half, (block + 1) * half)
        drive[:, block * whole : block * whole + half] = drive_straight[:, lanes]
        drive[:, block * whole + half : (block + 1) * whole] = drive_turned[:, lanes]

    load_inverse.wait()
    for k in range(iters):
        last = k == iters - 1
        lines = strip if last else slice(0, whole)
        cross[k].wait_recv()
        relay[k].start()
        if k + 2 < iters:
            core[k + 2].start()
        for part in range(2):
            block = column_bit if part == 0 else 1 - column_bit
            if part == 1:
                core[k].wait_recv()
                relay[k].wait_recv()
            build_green(k, block)
            lanes = pl.ds(pl.multiple_of(block * whole, whole), whole)
            product[k, lines, lanes] = mul(chain[lines, :], right_green[...]).astype(BF16)

        @pl.when(column_bit == 0)
        def _():
            share[k].start()

        for block in range(2):
            result = mul(product[k, lines, :], right_chain[k, block]).astype(BF16)
            if last:
                stage[block, 0] = result[:, :half]
                stage[block, 1] = result[:, half:]
            else:
                chain[:, block * whole : (block + 1) * whole] = result
        if last:
            forward_out = remote(
                stage.at[1], far_forward_ref.at[0], far_sems.at[0], far_sems.at[1], "rows", beside
            )
            backward_out = remote(
                stage.at[0], far_backward_ref.at[0], far_sems.at[0], far_sems.at[1], "rows", beside
            )
            forward_keep = pltpu.make_async_copy(
                stage.at[0], far_forward_ref.at[0], local_sems.at[2]
            )
            backward_keep = pltpu.make_async_copy(
                stage.at[1], far_backward_ref.at[0], local_sems.at[2]
            )

            @pl.when(column_bit == 0)
            def _():
                forward_out.start()
                forward_keep.start()

            @pl.when(column_bit == 1)
            def _():
                backward_out.start()
                backward_keep.start()
        else:
            build_chain(k + 1)

        @pl.when(column_bit == 1)
        def _():
            share[k].wait_recv()
            for block in range(2):
                lanes = slice(block * whole, (block + 1) * whole)
                term = mul(arrived[k], right_chain[k, block])
                if k == 0:
                    surface[:, lanes] = term
                else:
                    surface[:, lanes] += term

    def piece(target, send_sem):
        begin = pl.multiple_of(target * per_row, per_row)
        return remote(
            pieces.at[pl.ds(begin, per_row)],
            gathered.at[slot, row_bit],
            send_sem,
            piece_recv.at[2 * slot + row_bit],
            "rows",
            target,
        )

    @pl.when(column_bit == 1)
    def _():
        self_energy = surface[...].astype(BF16)
        pieces[...] = lax.dot_general(
            drive[...], self_energy, (((1,), (1,)), ((), ())), preferred_element_type=F32
        ).astype(BF16)
        for step in range(1, rows_size):
            piece(lax.rem(position + step, rows_size), piece_send.at[step]).start()
        begin = pl.multiple_of(position * per_row, per_row)
        keep = pltpu.make_async_copy(
            pieces.at[pl.ds(begin, per_row)], gathered.at[slot, row_bit], piece_send.at[0]
        )
        keep.start()
        keep.wait()

    for index in range(2 * groups):
        sender = index // 2 * 4 + index % 2 * 2 + 1

        @pl.when(position != sender)
        def _():
            remote(
                pieces.at[pl.ds(0, per_row)],
                gathered.at[index // 2, index % 2],
                piece_send.at[0],
                piece_recv.at[index],
                "rows",
                position,
            ).wait_recv()

    for line in range(2):
        columns = slice(line * half, (line + 1) * half)
        terms = [gathered[index, line].astype(F32) for index in range(groups)]
        total = jnp.zeros_like(terms[0])
        for group in range(groups):
            picked = jnp.zeros_like(total)
            for index in range(groups):
                mark = jnp.full(total.shape, lax.rem(assignment_ref[index], groups), jnp.int32)
                picked = jnp.where(mark == group, terms[index], picked)
            injection_ref[group, 0, :, :, columns] = picked.reshape(2, states_count, half)
            total = total + weights_ref[group] * picked
        weighted[:, columns] = total.astype(BF16)
        over_energy[energy, :, columns] = total.astype(BF16)

    sums = [
        remote(
            weighted,
            over_energy.at[energy],
            energy_send.at[step],
            energy_recv.at[energy],
            "energy",
            lax.rem(energy + step, energy_size),
        )
        for step in range(1, energy_size)
    ]
    for copy in sums:
        copy.start()
    for index in range(energy_size):

        @pl.when(energy != index)
        def _():
            remote(
                weighted,
                over_energy.at[index],
                energy_send.at[0],
                energy_recv.at[index],
                "energy",
                energy,
            ).wait_recv()

    for line in range(2):
        columns = slice(line * half, (line + 1) * half)
        total = over_energy[0, :, columns].astype(F32)
        for index in range(1, energy_size):
            total = total + over_energy[index, :, columns].astype(F32)
        integrated_ref[0, :, :, columns] = total.reshape(2, states_count, half)

    for copy in sums:
        copy.wait_send()
    for k in range(iters):
        cross[k].wait_send()
        core[k].wait_send()
        relay[k].wait_send()

    @pl.when(column_bit == 0)
    def _():
        for k in range(iters):
            share[k].wait_send()
        forward_keep.wait()
        forward_out.wait_send()
        backward_out.wait_recv()

    @pl.when(column_bit == 1)
    def _():
        for step in range(1, rows_size):
            piece(lax.rem(position + step, rows_size), piece_send.at[step]).wait_send()
        backward_keep.wait()
        backward_out.wait_send()
        forward_out.wait_recv()


def local(rows_size, energy_size, coupling, inverses, contact_row, assignment, states, weights):
    iters, half = inverses.shape[1], inverses.shape[-1]
    whole = 2 * half
    groups = assignment.shape[0]
    contacts, _, states_count, _ = states.shape
    per_row = 2 * states_count
    any_space = pl.BlockSpec(memory_space=pl.ANY)
    smem = pl.BlockSpec(memory_space=pltpu.SMEM)
    vmem = pl.BlockSpec(memory_space=pltpu.VMEM)
    dma = pltpu.SemaphoreType.DMA
    far = jax.ShapeDtypeStruct((1, 2, half, half), BF16)
    return pl.pallas_call(
        functools.partial(kernel, rows_size, energy_size),
        out_shape=(
            jax.ShapeDtypeStruct((groups, 1, 2, states_count, whole), F32),
            jax.ShapeDtypeStruct((1, 2, states_count, whole), F32),
            far,
            far,
        ),
        in_specs=[any_space, any_space, smem, smem, vmem, smem],
        out_specs=(vmem, vmem, any_space, any_space),
        scratch_shapes=[
            pltpu.VMEM((2, whole, whole), BF16),
            pltpu.VMEM((4, iters, 2, half, half), BF16),
            pltpu.VMEM((whole, 2 * whole), BF16),
            pltpu.VMEM((iters, whole, 2 * whole), BF16),
            pltpu.VMEM((iters, 2, 2 * whole, whole), BF16),
            pltpu.VMEM((2 * whole, whole), BF16),
            pltpu.VMEM((iters, half, 2 * whole), BF16),
            pltpu.VMEM((half, 2 * whole), F32),
            pltpu.VMEM((rows_size * per_row, 2 * whole), BF16),
            pltpu.VMEM((rows_size * per_row, half), BF16),
            pltpu.VMEM((groups, 2, per_row, half), BF16),
            pltpu.VMEM((per_row, whole), BF16),
            pltpu.VMEM((energy_size, per_row, whole), BF16),
            pltpu.VMEM((2, 2, half, half), BF16),
            dma((3,)),
            dma((2, iters)),
            dma((2, iters)),
            dma((2, iters)),
            dma((2, iters)),
            dma((2,)),
            dma((rows_size,)),
            dma((2 * groups,)),
            dma((energy_size,)),
            dma((energy_size,)),
        ],
        compiler_params=pltpu.CompilerParams(
            collective_id=0, has_side_effects=True, vmem_limit_bytes=60 * 1024 * 1024
        ),
        name="decimate",
    )(coupling, inverses, contact_row, assignment, states, weights)


def solution(mesh):
    rows_size, energy_size = mesh.shape["rows"], mesh.shape["energy"]
    placed = (
        P(),
        P(("energy", "rows"), None, None, None, None),
        P(),
        P("energy"),
        P(),
        P("energy"),
    )
    return jax.shard_map(
        functools.partial(local, rows_size, energy_size),
        mesh=mesh,
        in_specs=placed,
        out_specs=(
            P("energy", "rows", None, None, None),
            P("rows", None, None, None),
            P(("energy", "rows"), None, None, None),
            P(("energy", "rows"), None, None, None),
        ),
        check_vma=False,
    )
```

```python
import functools

import jax
import jax.numpy as jnp
from jax import lax
from jax.experimental import pallas as pl
from jax.experimental.pallas import tpu as pltpu
from jax.sharding import PartitionSpec as P

MESH = pl.DeviceIdType.MESH
BF16 = jnp.bfloat16
F32 = jnp.float32


def remote(src, dst, send_sem, recv_sem, axis, target):
    return pltpu.make_async_remote_copy(
        src_ref=src,
        dst_ref=dst,
        send_sem=send_sem,
        recv_sem=recv_sem,
        device_id={axis: target},
        device_id_type=MESH,
    )


def mul(left, right):
    return jnp.dot(left, right, preferred_element_type=F32)


def kernel(
    rows_size,
    energy_size,
    coupling_ref,
    inverses_ref,
    contact_ref,
    assignment_ref,
    states_ref,
    weights_ref,
    injection_ref,
    integrated_ref,
    far_forward_ref,
    far_backward_ref,
    held,
    blocks,
    chain,
    product,
    right_chain,
    right_green,
    arrived,
    surface,
    side,
    left_green,
    right_term,
    total_surface,
    states_held,
    drive,
    pieces,
    gathered,
    weighted,
    over_energy,
    stage,
    local_sems,
    cross_sems,
    core_sems,
    relay_sems,
    product_sems,
    far_sems,
    piece_send,
    piece_recv,
    energy_send,
    energy_recv,
):
    energy = lax.axis_index("energy")
    position = lax.axis_index("rows")
    iters = inverses_ref.shape[1]
    half = inverses_ref.shape[-1]
    whole = 2 * half
    groups = assignment_ref.shape[0]
    contacts, _, states_count, _ = states_ref.shape
    slot = position // 4
    row_bit = position // 2 % 2
    column_bit = position % 2
    across = slot * 4 + 2 * (1 - row_bit) + column_bit
    beside = slot * 4 + 2 * row_bit + 1 - column_bit
    own_block = 2 * row_bit + column_bit
    cross_block = 2 * (1 - row_bit) + column_bit

    load_coupling = pltpu.make_async_copy(coupling_ref, held, local_sems.at[0])
    load_coupling.start()
    load_inverse = pltpu.make_async_copy(
        inverses_ref.at[0], blocks.at[own_block], local_sems.at[1]
    )
    load_inverse.start()
    load_states = pltpu.make_async_copy(states_ref, states_held, local_sems.at[3])
    load_states.start()

    barrier = pltpu.get_barrier_semaphore()
    for step in range(1, rows_size):
        pl.semaphore_signal(
            barrier,
            inc=1,
            device_id={"rows": lax.rem(position + step, rows_size)},
            device_id_type=MESH,
        )
    for step in range(1, energy_size):
        pl.semaphore_signal(
            barrier,
            inc=1,
            device_id={"energy": lax.rem(energy + step, energy_size)},
            device_id_type=MESH,
        )
    pl.semaphore_wait(barrier, rows_size + energy_size - 2)

    cross = [
        remote(
            inverses_ref.at[0, k],
            blocks.at[own_block, k],
            cross_sems.at[0, k],
            cross_sems.at[1, k],
            "rows",
            across,
        )
        for k in range(iters)
    ]
    core = [
        remote(
            inverses_ref.at[0, k],
            blocks.at[own_block, k],
            core_sems.at[0, k],
            core_sems.at[1, k],
            "rows",
            beside,
        )
        for k in range(iters)
    ]
    relay = [
        remote(
            blocks.at[cross_block, k],
            blocks.at[cross_block, k],
            relay_sems.at[0, k],
            relay_sems.at[1, k],
            "rows",
            beside,
        )
        for k in range(iters)
    ]
    side_lanes = pl.ds(pl.multiple_of(row_bit * whole, whole), whole)
    strip = pl.ds(pl.multiple_of(row_bit * half, half), half)
    share = [
        remote(
            product.at[k, strip] if k < iters - 1 else chain.at[:, side_lanes],
            arrived.at[k] if k < iters - 1 else side,
            product_sems.at[0, k],
            product_sems.at[1, k],
            "rows",
            beside,
        )
        for k in range(iters)
    ]
    for k in range(iters):
        cross[k].start()
    for k in range(min(2, iters)):
        core[k].start()

    load_coupling.wait()

    def spread(part, index):
        for block in range(2):
            chain[:, pl.ds(block * whole + index * half, half)] = part[
                :, block * half : (block + 1) * half
            ]

    @pl.when(column_bit == 0)
    def _():
        spread(held[0], 0)
        spread(held[1], 1)

    @pl.when(column_bit == 1)
    def _():
        spread(held[0].T, 0)
        spread(-(held[1].T), 1)

    def build_chain(k):
        for block in range(2):
            for line in range(2):
                lines = slice(line * half, (line + 1) * half)
                real = chain[lines, block * whole : block * whole + half]
                imag = chain[lines, block * whole + half : (block + 1) * whole]
                top = line * whole
                right_chain[k, block, top : top + half, :half] = real
                right_chain[k, block, top : top + half, half:] = imag
                right_chain[k, block, top + half : top + whole, :half] = -imag
                right_chain[k, block, top + half : top + whole, half:] = real

    def build_green(k, block):
        for line in range(2):
            real = blocks[2 * line + block, k, 0]
            imag = blocks[2 * line + block, k, 1]
            top = line * whole
            right_green[top : top + half, :half] = real
            right_green[top : top + half, half:] = imag
            right_green[top + half : top + whole, :half] = -imag
            right_green[top + half : top + whole, half:] = real

    build_chain(0)

    per_row = 2 * states_count
    shift = per_row.bit_length() - 1
    shape = (rows_size * per_row, contacts * per_row)
    line_ids = lax.broadcasted_iota(jnp.int32, shape, 0)
    lane_ids = lax.broadcasted_iota(jnp.int32, shape, 1)
    lane_contact = lane_ids >> shift
    lane_row = jnp.zeros(shape, jnp.int32)
    for contact in range(contacts):
        lane_row = jnp.where(lane_contact == contact, contact_ref[contact], lane_row)
    chosen = lane_row == (line_ids >> shift)
    line_item = line_ids & (per_row - 1)
    lane_item = lane_ids & (per_row - 1)
    load_states.wait()
    flat_states = states_held[...].reshape(contacts * per_row, whole)
    straight = jnp.where(chosen & (line_item == lane_item), 1.0, 0.0).astype(BF16)
    turned_item = (line_item + states_count) & (per_row - 1)
    sign = jnp.where(line_item < states_count, -1.0, 1.0)
    turned = jnp.where(chosen & (turned_item == lane_item), sign, 0.0).astype(BF16)
    drive_straight = mul(straight, flat_states).astype(BF16)
    drive_turned = mul(turned, flat_states).astype(BF16)
    for block in range(2):
        lanes = slice(block * half, (block + 1) * half)
        drive[:, block * whole : block * whole + half] = drive_straight[:, lanes]
        drive[:, block * whole + half : (block + 1) * whole] = drive_turned[:, lanes]

    def piece(target, send_sem):
        begin = pl.multiple_of(target * per_row, per_row)
        return remote(
            pieces.at[pl.ds(begin, per_row)],
            gathered.at[slot, row_bit],
            send_sem,
            piece_recv.at[2 * slot + row_bit],
            "rows",
            target,
        )

    def finish_surface():
        k = iters - 1
        core[k].wait_recv()
        pl.when(column_bit == 1)(close_surface)

    def close_surface():
        k = iters - 1
        for block in range(2):
            for index in range(2):
                lanes = slice(block * whole + index * half, block * whole + (index + 1) * half)
                left_green[:, lanes] = blocks[2 * row_bit + block, k, index]
        for block in range(2):
            term = mul(left_green[...], right_chain[k, block]).astype(BF16)
            real, imag = term[:, :half], term[:, half:]
            right_term[block, :half, :half] = real
            right_term[block, :half, half:] = imag
            right_term[block, half:, :half] = -imag
            right_term[block, half:, half:] = real
        share[k].wait_recv()
        for line in range(2):
            lines = slice(line * half, (line + 1) * half)
            for block in range(2):
                lanes = slice(block * whole, (block + 1) * whole)
                term = mul(side[lines, :], right_term[block])
                before = jnp.where(row_bit == line, surface[:, lanes], 0.0)
                total_surface[lines, lanes] = (term + before).astype(BF16)
        pieces[...] = lax.dot_general(
            drive[...], total_surface[...], (((1,), (1,)), ((), ())), preferred_element_type=F32
        ).astype(BF16)
        for step in range(1, rows_size):
            piece(lax.rem(position + step, rows_size), piece_send.at[step]).start()
        begin = pl.multiple_of(position * per_row, per_row)
        keep = pltpu.make_async_copy(
            pieces.at[pl.ds(begin, per_row)], gathered.at[slot, row_bit], piece_send.at[0]
        )
        keep.start()
        keep.wait()

    def gather():
        for index in range(2 * groups):
            sender = index // 2 * 4 + index % 2 * 2 + 1

            @pl.when(position != sender)
            def _():
                remote(
                    pieces.at[pl.ds(0, per_row)],
                    gathered.at[index // 2, index % 2],
                    piece_send.at[0],
                    piece_recv.at[index],
                    "rows",
                    position,
                ).wait_recv()

        for line in range(2):
            columns = slice(line * half, (line + 1) * half)
            terms = [
                gathered[index, 0, :, columns].astype(F32) + gathered[index, 1, :, columns].astype(F32)
                for index in range(groups)
            ]
            total = jnp.zeros_like(terms[0])
            for group in range(groups):
                picked = jnp.zeros_like(total)
                for index in range(groups):
                    mark = jnp.full(total.shape, lax.rem(assignment_ref[index], groups), jnp.int32)
                    picked = jnp.where(mark == group, terms[index], picked)
                injection_ref[group, 0, :, :, columns] = picked.reshape(2, states_count, half)
                total = total + weights_ref[group] * picked
            weighted[:, columns] = total.astype(BF16)
            over_energy[energy, :, columns] = total.astype(BF16)

        sums = [
            remote(
                weighted,
                over_energy.at[energy],
                energy_send.at[step],
                energy_recv.at[energy],
                "energy",
                lax.rem(energy + step, energy_size),
            )
            for step in range(1, energy_size)
        ]
        for copy in sums:
            copy.start()
        return sums

    load_inverse.wait()
    for k in range(iters):
        last = k == iters - 1
        lines = strip if last else slice(0, whole)
        if last:
            finish_surface()
        cross[k].wait_recv()
        relay[k].start()
        if k + 2 < iters:
            core[k + 2].start()
        for part in range(2):
            block = column_bit if part == 0 else 1 - column_bit
            if part == 1:
                if not last:
                    core[k].wait_recv()
                relay[k].wait_recv()
            build_green(k, block)
            lanes = pl.ds(pl.multiple_of(block * whole, whole), whole)
            product[k, lines, lanes] = mul(chain[lines, :], right_green[...]).astype(BF16)

        if not last:

            @pl.when(column_bit == 0)
            def _():
                share[k].start()

        if last:
            sums = gather()
        for block in range(2):
            result = mul(product[k, lines, :], right_chain[k, block]).astype(BF16)
            if last:
                stage[block, 0] = result[:, :half]
                stage[block, 1] = result[:, half:]
            else:
                chain[:, block * whole : (block + 1) * whole] = result
        if last:
            forward_out = remote(
                stage.at[1], far_forward_ref.at[0], far_sems.at[0], far_sems.at[1], "rows", beside
            )
            backward_out = remote(
                stage.at[0], far_backward_ref.at[0], far_sems.at[0], far_sems.at[1], "rows", beside
            )
            forward_keep = pltpu.make_async_copy(
                stage.at[0], far_forward_ref.at[0], local_sems.at[2]
            )
            backward_keep = pltpu.make_async_copy(
                stage.at[1], far_backward_ref.at[0], local_sems.at[2]
            )

            @pl.when(column_bit == 0)
            def _():
                forward_out.start()
                forward_keep.start()

            @pl.when(column_bit == 1)
            def _():
                backward_out.start()
                backward_keep.start()
        else:
            if k == iters - 2:

                @pl.when(column_bit == 0)
                def _():
                    share[k + 1].start()

            build_chain(k + 1)

            @pl.when(column_bit == 1)
            def _():
                share[k].wait_recv()
                for block in range(2):
                    lanes = slice(block * whole, (block + 1) * whole)
                    term = mul(arrived[k], right_chain[k, block])
                    if k == 0:
                        surface[:, lanes] = term
                    else:
                        surface[:, lanes] += term

    for index in range(energy_size):

        @pl.when(energy != index)
        def _():
            remote(
                weighted,
                over_energy.at[index],
                energy_send.at[0],
                energy_recv.at[index],
                "energy",
                energy,
            ).wait_recv()

    for line in range(2):
        columns = slice(line * half, (line + 1) * half)
        total = over_energy[0, :, columns].astype(F32)
        for index in range(1, energy_size):
            total = total + over_energy[index, :, columns].astype(F32)
        integrated_ref[0, :, :, columns] = total.reshape(2, states_count, half)

    for copy in sums:
        copy.wait_send()
    for k in range(iters):
        cross[k].wait_send()
        core[k].wait_send()
        relay[k].wait_send()

    @pl.when(column_bit == 0)
    def _():
        for k in range(iters):
            share[k].wait_send()
        forward_keep.wait()
        forward_out.wait_send()
        backward_out.wait_recv()

    @pl.when(column_bit == 1)
    def _():
        for step in range(1, rows_size):
            piece(lax.rem(position + step, rows_size), piece_send.at[step]).wait_send()
        backward_keep.wait()
        backward_out.wait_send()
        forward_out.wait_recv()


def deliver(*refs):
    count = len(refs) // 2
    sems = refs[-1]
    copies = [
        pltpu.make_async_copy(refs[index], refs[count + index], sems.at[index])
        for index in range(count)
    ]
    for copy in copies:
        copy.start()
    for copy in copies:
        copy.wait()


def local(rows_size, energy_size, coupling, inverses, contact_row, assignment, states, weights):
    iters, half = inverses.shape[1], inverses.shape[-1]
    whole = 2 * half
    groups = assignment.shape[0]
    contacts, _, states_count, _ = states.shape
    per_row = 2 * states_count
    any_space = pl.BlockSpec(memory_space=pl.ANY)
    hbm = pl.BlockSpec(memory_space=pltpu.HBM)
    smem = pl.BlockSpec(memory_space=pltpu.SMEM)
    vmem = pl.BlockSpec(memory_space=pltpu.VMEM)
    dma = pltpu.SemaphoreType.DMA
    far = jax.ShapeDtypeStruct((1, 2, half, half), BF16)
    coupling, inverses, contact_row, assignment, states, weights = (
        pltpu.with_memory_space_constraint(item, pltpu.HBM)
        for item in (coupling, inverses, contact_row, assignment, states, weights)
    )
    outputs = pl.pallas_call(
        functools.partial(kernel, rows_size, energy_size),
        out_shape=(
            jax.ShapeDtypeStruct((groups, 1, 2, states_count, whole), F32),
            jax.ShapeDtypeStruct((1, 2, states_count, whole), F32),
            far,
            far,
        ),
        in_specs=[hbm, hbm, smem, smem, hbm, smem],
        out_specs=(vmem, vmem, any_space, any_space),
        scratch_shapes=[
            pltpu.VMEM((2, whole, whole), BF16),
            pltpu.VMEM((4, iters, 2, half, half), BF16),
            pltpu.VMEM((whole, 2 * whole), BF16),
            pltpu.VMEM((iters, whole, 2 * whole), BF16),
            pltpu.VMEM((iters, 2, 2 * whole, whole), BF16),
            pltpu.VMEM((2 * whole, whole), BF16),
            pltpu.VMEM((iters - 1, half, 2 * whole), BF16),
            pltpu.VMEM((half, 2 * whole), F32),
            pltpu.VMEM((whole, whole), BF16),
            pltpu.VMEM((half, 2 * whole), BF16),
            pltpu.VMEM((2, whole, whole), BF16),
            pltpu.VMEM((whole, 2 * whole), BF16),
            pltpu.VMEM(states.shape, BF16),
            pltpu.VMEM((rows_size * per_row, 2 * whole), BF16),
            pltpu.VMEM((rows_size * per_row, whole), BF16),
            pltpu.VMEM((groups, 2, per_row, whole), BF16),
            pltpu.VMEM((per_row, whole), BF16),
            pltpu.VMEM((energy_size, per_row, whole), BF16),
            pltpu.VMEM((2, 2, half, half), BF16),
            dma((4,)),
            dma((2, iters)),
            dma((2, iters)),
            dma((2, iters)),
            dma((2, iters)),
            dma((2,)),
            dma((rows_size,)),
            dma((2 * groups,)),
            dma((energy_size,)),
            dma((energy_size,)),
        ],
        compiler_params=pltpu.CompilerParams(
            collective_id=0, has_side_effects=True, vmem_limit_bytes=36 * 1024 * 1024
        ),
        name="decimate",
    )(coupling, inverses, contact_row, assignment, states, weights)
    return pl.pallas_call(
        deliver,
        out_shape=tuple(jax.ShapeDtypeStruct(item.shape, item.dtype) for item in outputs),
        in_specs=[vmem] * len(outputs),
        out_specs=(hbm,) * len(outputs),
        scratch_shapes=[dma((len(outputs),))],
        compiler_params=pltpu.CompilerParams(vmem_limit_bytes=8 * 1024 * 1024),
        name="deliver",
    )(*outputs)


def solution(mesh):
    rows_size, energy_size = mesh.shape["rows"], mesh.shape["energy"]
    placed = (
        P(),
        P(("energy", "rows"), None, None, None, None),
        P(),
        P("energy"),
        P(),
        P("energy"),
    )
    return jax.shard_map(
        functools.partial(local, rows_size, energy_size),
        mesh=mesh,
        in_specs=placed,
        out_specs=(
            P("energy", "rows", None, None, None),
            P("rows", None, None, None),
            P(("energy", "rows"), None, None, None),
            P(("energy", "rows"), None, None, None),
        ),
        check_vma=False,
    )
```
